32 devices in a mesh: head: 4 (over y, x), vocab: 8 (over z, core).
Axes of the slice: x: 2, y: 2, z: 4, core: 2. Of those that a mesh axis runs over, the one named last changes fastest.
Arguments:
- hidden_rows: bfloat16 [512, 2048], P(('head', 'vocab')), may hold values from -240 to 240
- head_weight: bfloat16 [4, 2048, 16384], P('head', None, 'vocab'), may hold values from -0.125 to 0.125
- teacher_logits: bfloat16 [4, 512, 16384], P('head', 'vocab'), may hold values from -24 to 336
Outputs:
- weight_grad: bfloat16 [4, 2048, 16384], P('head', None, 'vocab')
- input_grad: float32 [512, 2048], P(('head', 'vocab'))
The draws below stay inside these ranges and needn't reach their ends.
All inputs are finite; a program needn't handle non-finite values.
Results may differ from the reference program's by a relative error of at most 0.004.
Values may be sent and summed in bfloat16 or wider, within the bound.
No kernel may reach another device: no remote copies, remote signals or barrier semaphores. Data moves between devices by JAX's collectives and lax.ppermute only.
A program may use at most 128 MiB of HBM per device.

```python
import jax
import jax.numpy as jnp
from jax import lax

D = 2048
TOK = 512
VOCAB = 16384
HEADS = 4


def draw_hidden_rows(key, part):
    first_key, second_key = jax.random.split(key)
    values = jnp.clip(jax.random.normal(first_key, (TOK, D), jnp.float32), -6.0, 6.0)
    scales = jnp.exp(jax.random.uniform(second_key, (TOK, 1), jnp.float32, jnp.log(3.0), jnp.log(30.0)))
    return (values * scales).astype(jnp.bfloat16)


def draw_teacher_logits(key, part):
    first_key = jax.random.fold_in(key, 0)
    values = 3.0 * jnp.clip(jax.random.normal(first_key, (HEADS, TOK, VOCAB), jnp.float32), -8.0, 8.0)
    return values.astype(jnp.bfloat16)


def steps_of(stream_key, dims, cuts, least, high):
    factor_of = 1.0
    for axis_at, parts in cuts:
        steps = jax.random.uniform(jax.random.fold_in(jax.random.fold_in(stream_key, 6), axis_at), (parts,), jnp.float32, least / len(cuts), high / len(cuts))
        factor_of = factor_of * jnp.repeat(jnp.exp(steps), dims[axis_at] // parts).reshape((-1,) + (1,) * (len(dims) - 1 - axis_at))
    return factor_of


def gaussian(rng, shape, spread, limit, cuts=(), dtype=jnp.bfloat16):
    gain = steps_of(rng, shape, cuts, -0.22, 0.18) if cuts else 1.0
    result = jax.random.normal(rng, shape, jnp.float32) * spread * gain
    return jnp.minimum(jnp.maximum(result, -limit), limit).astype(dtype)


def setup_inputs(seed: int = 0) -> dict:
    key_of = jax.random.split(jax.random.key(seed), 4)
    hidden_rows = draw_hidden_rows(jax.random.fold_in(key_of[3], 71), 0)
    head_weight = gaussian(key_of[1], (HEADS, D, VOCAB), D ** -0.5, 0.125, ((0, 4), (2, 8)))
    teacher_logits = draw_teacher_logits(jax.random.fold_in(key_of[3], 71), 0)
    return dict(hidden_rows=hidden_rows, head_weight=head_weight, teacher_logits=teacher_logits)


def reference(hidden_rows, head_weight, teacher_logits):
    def per_head(pair):
        weight, teacher = pair
        student = jnp.dot(hidden_rows, weight, preferred_element_type=jnp.float32)
        student_prob = jax.nn.softmax(student, axis=1)
        teacher_prob = jax.nn.softmax(teacher.astype(jnp.float32), axis=1)
        logit_grad = (student_prob - teacher_prob).astype(jnp.bfloat16)
        weight_grad = jnp.dot(hidden_rows.T, logit_grad, preferred_element_type=jnp.float32).astype(jnp.bfloat16)
        grad_part = jnp.dot(logit_grad, weight.T, preferred_element_type=jnp.float32)
        return weight_grad, grad_part

    weight_grad, grad_parts = lax.map(per_head, (head_weight, teacher_logits))
    return weight_grad, jnp.sum(grad_parts, axis=0)
```

```python
import functools

import jax
import jax.numpy as jnp
from jax import lax
from jax.experimental import pallas as pl
from jax.experimental.pallas import tpu as pltpu
from jax.sharding import PartitionSpec as P


F32 = jnp.float32
BF16 = jnp.bfloat16
LANES = 128
VMEM_LIMIT = 60 * 1024 * 1024
NT = (((1,), (1,)), ((), ()))
TN = (((0,), (0,)), ((), ()))


def params():
    return pltpu.CompilerParams(vmem_limit_bytes=VMEM_LIMIT)


def cost(flops, nbytes):
    return pl.CostEstimate(flops=flops, bytes_accessed=nbytes, transcendentals=0)


def teacher_stats_kernel(t_ref, o_ref, m_sc, l_sc):
    step = pl.program_id(0)
    x = t_ref[0].astype(F32)

    @pl.when(step == 0)
    def _():
        m_sc[...] = jnp.full_like(m_sc, -jnp.inf)
        l_sc[...] = jnp.zeros_like(l_sc)

    top = jnp.maximum(m_sc[...], jnp.max(x, axis=1, keepdims=True))
    l_sc[...] = l_sc[...] * jnp.exp(m_sc[...] - top) + jnp.sum(
        jnp.exp(x - top), axis=1, keepdims=True
    )
    m_sc[...] = top

    @pl.when(step == pl.num_programs(0) - 1)
    def _():
        lane = lax.broadcasted_iota(jnp.int32, o_ref.shape, 1)
        o_ref[...] = jnp.where(lane == 2, m_sc[...], jnp.where(lane == 3, l_sc[...], 0.0))


def teacher_stats(teacher, tile):
    _, rows, cols = teacher.shape
    return pl.pallas_call(
        teacher_stats_kernel,
        grid=(cols // tile,),
        in_specs=[pl.BlockSpec((1, rows, tile), lambda j: (0, 0, j))],
        out_specs=pl.BlockSpec((rows, LANES), lambda j: (0, 0)),
        out_shape=jax.ShapeDtypeStruct((rows, LANES), F32),
        scratch_shapes=[pltpu.VMEM((rows, 1), F32), pltpu.VMEM((rows, 1), F32)],
        compiler_params=params(),
        cost_estimate=cost(4 * rows * cols, 2 * rows * cols),
        name="teacher_stats",
    )(teacher)


def student_kernel(place, ids, tstat_ref, *refs):
    parts = refs[: place.pieces]
    w_ref, s_ref, h_ref, stat_ref, m_sc, l_sc, cols_sc, sem = refs[place.pieces :]
    step = pl.program_id(0)
    rows = parts[0].shape[0]
    me = ids[0] * place.nv + ids[1]

    @pl.when(step == 0)
    def _():
        for i, part in enumerate(parts):
            pltpu.make_async_copy(part, h_ref.at[pl.ds(i * rows, rows)], sem.at[i]).start()
        m_sc[...] = jnp.full_like(m_sc, -jnp.inf)
        l_sc[...] = jnp.zeros_like(l_sc)
        for i, part in enumerate(parts):
            pltpu.make_async_copy(part, h_ref.at[pl.ds(i * rows, rows)], sem.at[i]).wait()

    s = jnp.dot(h_ref[...], w_ref[...], preferred_element_type=F32)
    s_ref[...] = s
    top = jnp.maximum(m_sc[...], jnp.max(s, axis=1, keepdims=True))
    l_sc[...] = l_sc[...] * jnp.exp(m_sc[...] - top) + jnp.sum(
        jnp.exp(s - top), axis=1, keepdims=True
    )
    m_sc[...] = top

    @pl.when(step == pl.num_programs(0) - 1)
    def _():
        lane = lax.broadcasted_iota(jnp.int32, (place.group, LANES), 1)
        for r in range(place.groups):
            at = pl.ds(r * place.group, place.group)
            to = jnp.bitwise_xor(me, place.bits(r)) * place.group
            cols_sc[pl.ds(pl.multiple_of(to, place.group), place.group), :] = jnp.where(
                lane == 0, m_sc[at, :], jnp.where(lane == 1, l_sc[at, :], 0.0)
            )
        mine = pl.ds(pl.multiple_of(ids[1] * tstat_ref.shape[0], place.group), tstat_ref.shape[0])
        cols_sc[mine, :] = cols_sc[mine, :] + tstat_ref[...]
        stat_ref[...] = cols_sc[...].T[:8, :]


def student(place, ids, tstat, parts, weight, tile):
    depth, cols = weight.shape
    rows = sum(p.shape[0] for p in parts)
    full = lambda *_: (0, 0)
    return pl.pallas_call(
        functools.partial(student_kernel, place),
        grid_spec=pltpu.PrefetchScalarGridSpec(
            num_scalar_prefetch=1,
            grid=(cols // tile,),
            in_specs=[pl.BlockSpec(tstat.shape, full)]
            + [pl.BlockSpec(memory_space=pl.ANY)] * len(parts)
            + [pl.BlockSpec((depth, tile), lambda j, _: (0, j))],
            out_specs=[
                pl.BlockSpec((rows, tile), lambda j, _: (0, j)),
                pl.BlockSpec((rows, depth), full),
                pl.BlockSpec((8, rows), full),
            ],
            scratch_shapes=[
                pltpu.VMEM((rows, 1), F32),
                pltpu.VMEM((rows, 1), F32),
                pltpu.VMEM((rows, LANES), F32),
                pltpu.SemaphoreType.DMA((len(parts),)),
            ],
        ),
        out_shape=[
            jax.ShapeDtypeStruct((rows, cols), F32),
            jax.ShapeDtypeStruct((rows, depth), BF16),
            jax.ShapeDtypeStruct((8, rows), F32),
        ],
        compiler_params=params(),
        cost_estimate=cost(2 * rows * cols * depth, 2 * depth * cols + 4 * rows * cols),
        name="student",
    )(ids, tstat, *parts, weight)


def logit_grad_kernel(place, n_stats, ids, *refs):
    stats = refs[:n_stats]
    teachers = refs[n_stats : n_stats + place.nv]
    s_ref, g_ref, cols_sc = refs[n_stats + place.nv :]
    me = ids[0] * place.nv + ids[1]

    @pl.when(pl.program_id(0) == 0)
    def _():
        rows = [ref[at : at + 8, :] for ref in stats for at in range(0, ref.shape[0], 8)]
        top = functools.reduce(jnp.maximum, [r[0:1] for r in rows])
        total = sum(r[1:2] * jnp.exp(r[0:1] - top) for r in rows)
        teacher_top = sum(r[2:3] for r in rows)
        teacher_total = sum(r[3:4] for r in rows)
        packed = jnp.concatenate(
            [top, 1.0 / total, teacher_top, 1.0 / teacher_total]
            + [jnp.zeros((LANES - 4, top.shape[1]), F32)],
            axis=0,
        )
        cols_sc[...] = packed.T

    for vk, t_ref in enumerate(teachers):
        per = t_ref.shape[0] // place.group
        for sub in range(per):
            can = jnp.bitwise_xor(ids[1], vk) * per + sub
            at = pl.ds(pl.multiple_of(can * place.group, place.group), place.group)
            c = cols_sc[at, :]
            to = place.position(jnp.bitwise_xor(me, can)) * place.group
            to = pl.ds(pl.multiple_of(to, place.group), place.group)
            t = t_ref[sub * place.group : (sub + 1) * place.group, :].astype(F32)
            p = jnp.exp(s_ref[to, :] - c[:, 0:1]) * c[:, 1:2]
            q = jnp.exp(t - c[:, 2:3]) * c[:, 3:4]
            g_ref[to, :] = (p - q).astype(BF16)


def logit_grad(place, ids, stats, teachers, s, tile):
    rows, cols = s.shape
    full = lambda *_: (0, 0)
    return pl.pallas_call(
        functools.partial(logit_grad_kernel, place, len(stats)),
        grid_spec=pltpu.PrefetchScalarGridSpec(
            num_scalar_prefetch=1,
            grid=(cols // tile,),
            in_specs=[pl.BlockSpec(x.shape, full) for x in stats]
            + [pl.BlockSpec((t.shape[0], tile), lambda j, _: (0, j)) for t in teachers]
            + [pl.BlockSpec((rows, tile), lambda j, _: (0, j))],
            out_specs=pl.BlockSpec((rows, tile), lambda j, _: (0, j)),
            scratch_shapes=[pltpu.VMEM((rows, LANES), F32)],
        ),
        out_shape=jax.ShapeDtypeStruct((rows, cols), BF16),
        compiler_params=params(),
        cost_estimate=cost(8 * rows * cols, 8 * rows * cols),
        name="logit_grad",
    )(ids, *stats, *teachers, s)


def input_grad_kernel(g_ref, w_ref, keep_ref, send_ref):
    out = lax.dot_general(g_ref[...], w_ref[...], NT, preferred_element_type=F32)
    half = out.shape[0] // 2
    keep_ref[...] = out[:half]
    send_ref[...] = out[half:].astype(BF16)


def input_grad_part(g, weight, start, width, tile):
    rows, cols = g.shape
    return pl.pallas_call(
        input_grad_kernel,
        grid=(width // tile,),
        in_specs=[
            pl.BlockSpec((rows, cols), lambda j: (0, 0)),
            pl.BlockSpec((tile, cols), lambda j: (start // tile + j, 0)),
        ],
        out_specs=[
            pl.BlockSpec((rows // 2, tile), lambda j: (0, j)),
            pl.BlockSpec((rows // 2, tile), lambda j: (0, j)),
        ],
        out_shape=[
            jax.ShapeDtypeStruct((rows // 2, width), F32),
            jax.ShapeDtypeStruct((rows // 2, width), BF16),
        ],
        compiler_params=params(),
        cost_estimate=cost(2 * rows * cols * width, 2 * cols * (rows + width)),
        name="input_grad",
    )(g, weight)


def weight_grad_kernel(h_ref, g_ref, o_ref, ht_sc):
    @pl.when(pl.program_id(0) == 0)
    def _():
        ht_sc[...] = h_ref[...].T

    o_ref[0] = jnp.dot(ht_sc[...], g_ref[...], preferred_element_type=F32).astype(BF16)


def weight_grad(h, g, tile):
    rows, depth = h.shape
    cols = g.shape[1]
    return pl.pallas_call(
        weight_grad_kernel,
        grid=(cols // tile,),
        in_specs=[
            pl.BlockSpec((rows, depth), lambda j: (0, 0)),
            pl.BlockSpec((rows, tile), lambda j: (0, j)),
        ],
        out_specs=pl.BlockSpec((1, depth, tile), lambda j: (0, 0, j)),
        out_shape=jax.ShapeDtypeStruct((1, depth, cols), BF16),
        scratch_shapes=[pltpu.VMEM((depth, rows), BF16)],
        compiler_params=params(),
        cost_estimate=cost(2 * rows * cols * depth, 2 * depth * cols),
        name="weight_grad",
    )(h, g)


class Place:
    def __init__(self, nh, nv, group):
        self.nh, self.nv, self.nz, self.group = nh, nv, nv // 2, group
        self.groups = nh * nv
        self.pieces = nh * 2

    def bits(self, r):
        ck, rest = divmod(r, self.nh * self.nz)
        hk, zk = divmod(rest, self.nz)
        return hk * self.nv + zk * 2 + ck

    def position(self, d):
        hk, vk = d // self.nv, d % self.nv
        zk, ck = vk // 2, vk % 2
        return (ck * self.nh + hk) * self.nz + zk


def swap(x, axis, size, k):
    return lax.ppermute(x, axis, [(i, i ^ k) for i in range(size)])


def relative(nh, nv, hidden, weight, teacher):
    place = Place(nh, nv, hidden.shape[0])
    nz = place.nz
    v = lax.axis_index("vocab")
    ids = jnp.stack([lax.axis_index("head"), v]).astype(jnp.int32)
    cols = weight.shape[2]

    near = [hidden] + [swap(hidden, "vocab", nv, 2 * k) for k in range(1, nz)]
    block = jnp.concatenate(near, axis=0)
    own = [block] + [swap(block, "head", nh, k) for k in range(1, nh)]
    other = [swap(x, "vocab", nv, 1) for x in own]

    def piece(k):
        return lax.dynamic_slice(
            teacher, (0, 0, (v ^ k) * cols), (1, teacher.shape[1], cols)
        )[0]

    mine = [piece(2 * k) for k in range(nz)]
    cross = [swap(piece(2 * k + 1), "vocab", nv, 1) for k in range(nz)]
    blocks = [None] * nv
    blocks[0], blocks[1] = mine[0], cross[0]
    for k in range(1, nz):
        blocks[2 * k] = swap(mine[k], "vocab", nv, 2 * k)
    for k in range(1, nz):
        blocks[2 * k + 1] = swap(cross[k], "vocab", nv, 2 * k)

    tstat = teacher_stats(teacher, teacher.shape[2] // 8)
    s, h, stat = student(place, ids, tstat, own + other, weight[0], 256)
    pair = jnp.concatenate([stat, swap(stat, "vocab", nv, 1)], axis=0)
    stats = [pair] + [swap(pair, "vocab", nv, 2 * k) for k in range(1, nz)]
    g = logit_grad(place, ids, stats, blocks, s, 512)

    depth = weight.shape[1]
    chunks = 2
    width = depth // chunks
    rows = place.group * nz
    sums = []
    for c in range(chunks):
        keep, send = input_grad_part(g, weight[0], c * width, width, 256)
        keep = keep + swap(send, "vocab", nv, 1).astype(F32)
        part = [keep[k * rows : (k + 1) * rows] for k in range(nh)]
        total = part[0]
        for k in range(1, nh):
            total = total + swap(part[k].astype(BF16), "head", nh, k).astype(F32)
        part = [total[k * place.group : (k + 1) * place.group] for k in range(nz)]
        total = part[0]
        for k in range(1, nz):
            total = total + swap(part[k].astype(BF16), "vocab", nv, 2 * k).astype(F32)
        sums.append(total)
    return (weight_grad(h, g, 256), jnp.concatenate(sums, axis=1))


def gathered(nh, nv, hidden, weight, teacher):
    trunk = lax.all_gather(hidden, ("head", "vocab"), axis=0, tiled=True)
    weight = weight[0]
    teacher = lax.all_to_all(teacher, "vocab", split_axis=2, concat_axis=1, tiled=True)[0]
    teacher = teacher.astype(F32)
    s = jnp.dot(trunk, weight, preferred_element_type=F32)
    tops = [jnp.max(x, axis=1) for x in (s, teacher)]
    totals = [jnp.sum(jnp.exp(x - m[:, None]), axis=1) for x, m in zip((s, teacher), tops)]
    stat = lax.all_gather(jnp.stack(tops + totals), "vocab")
    prob = []
    for i, x in enumerate((s, teacher)):
        top = jnp.max(stat[:, i], axis=0)
        total = jnp.sum(stat[:, i + 2] * jnp.exp(stat[:, i] - top), axis=0)
        prob.append(jnp.exp(x - top[:, None]) / total[:, None])
    g = (prob[0] - prob[1]).astype(BF16)
    grad = lax.dot_general(trunk, g, TN, preferred_element_type=F32).astype(BF16)[None]
    back = lax.dot_general(g, weight, NT, preferred_element_type=F32)
    return (grad, lax.psum_scatter(back, ("head", "vocab"), scatter_dimension=0, tiled=True))


def per_device(nh, nv, hidden, weight, teacher):
    two_powers = nh & (nh - 1) == 0 and nv & (nv - 1) == 0
    form = relative if two_powers and hidden.shape[0] % 16 == 0 else gathered
    return form(nh, nv, hidden, weight, teacher)


def solution(mesh):
    return jax.shard_map(
        functools.partial(per_device, mesh.shape["head"], mesh.shape["vocab"]),
        mesh=mesh,
        in_specs=(P(("head", "vocab"), None), P("head", None, "vocab"), P("head", "vocab", None)),
        out_specs=(P("head", None, "vocab"), P(("head", "vocab"), None)),
        check_vma=False,
    )
```

```python
import functools

import jax
import jax.numpy as jnp
from jax import lax
from jax.experimental import pallas as pl
from jax.experimental.pallas import tpu as pltpu
from jax.sharding import PartitionSpec as P


F32 = jnp.float32
BF16 = jnp.bfloat16
LANES = 128
NT = (((1,), (1,)), ((), ()))
TN = (((0,), (0,)), ((), ()))
MIB = 1024 * 1024


def params(nbytes):
    return pltpu.CompilerParams(vmem_limit_bytes=nbytes + 4 * MIB)


def cost(flops, nbytes):
    return pl.CostEstimate(flops=flops, bytes_accessed=nbytes, transcendentals=0)


WHOLE = pl.BlockSpec(memory_space=pltpu.VMEM)


def teacher_stats(teacher):
    x = teacher[0].astype(F32)
    top = jnp.max(x, axis=1)
    return jnp.stack([top, jnp.sum(jnp.exp(x - top[:, None]), axis=1)])


def stack_kernel(*refs):
    rows = refs[0].shape[0]
    for i, ref in enumerate(refs[:-1]):
        refs[-1][i * rows : (i + 1) * rows, :] = ref[...]


def stacked(parts):
    rows, cols = parts[0].shape
    shape = jax.ShapeDtypeStruct((rows * len(parts), cols), parts[0].dtype)
    nbytes = shape.size * shape.dtype.itemsize
    return pl.pallas_call(
        stack_kernel,
        in_specs=[WHOLE] * len(parts),
        out_specs=WHOLE,
        out_shape=shape,
        compiler_params=params(2 * nbytes),
        cost_estimate=cost(0, 2 * nbytes),
    )(*parts)


def student_kernel(pieces, tile, *refs):
    parts, (w_ref, t_ref, e_ref, h_ref, stat_ref, cols_sc) = refs[:pieces], refs[pieces:]
    rows = parts[0].shape[0]
    for i, part in enumerate(parts):
        h_ref[i * rows : (i + 1) * rows, :] = part[...]

    @pl.loop(0, w_ref.shape[1] // tile)
    def _(j):
        at = pl.ds(pl.multiple_of(j * tile, tile), tile)
        e_ref[:, at] = jnp.dot(h_ref[...], w_ref[:, at], preferred_element_type=F32)

    step = 8
    lane = lax.broadcasted_iota(jnp.int32, (step, LANES), 1)

    def body(i, _):
        at = pl.ds(pl.multiple_of(i * step, step), step)
        x = e_ref[at, :]
        top = jnp.max(x, axis=1, keepdims=True)
        e = jnp.exp(x - top)
        e_ref[at, :] = e
        total = jnp.sum(e, axis=1, keepdims=True)
        cols_sc[at, :] = jnp.where(lane == 0, top, jnp.where(lane == 1, total, 0.0))
        return _

    lax.fori_loop(0, e_ref.shape[0] // step, body, 0, unroll=4)
    stat_ref[...] = cols_sc[...].T[:8, :]
    stat_ref[2:4, : t_ref.shape[1]] = t_ref[...]


def student(parts, weight, tstat, tile):
    depth, cols = weight.shape
    rows = sum(p.shape[0] for p in parts)
    return pl.pallas_call(
        functools.partial(student_kernel, len(parts), tile),
        in_specs=[WHOLE] * (len(parts) + 2),
        out_specs=[WHOLE] * 3,
        out_shape=[
            jax.ShapeDtypeStruct((rows, cols), F32),
            jax.ShapeDtypeStruct((rows, depth), BF16),
            jax.ShapeDtypeStruct((8, rows), F32),
        ],
        scratch_shapes=[pltpu.VMEM((rows, LANES), F32)],
        compiler_params=params(2 * depth * cols + 8 * rows * cols + 4 * rows * depth),
        cost_estimate=cost(2 * rows * cols * depth, 2 * depth * cols + 4 * rows * cols),
        name="student",
    )(*parts, weight, tstat)


def swap_groups(x, size, lanes):
    lane = lax.broadcasted_iota(jnp.int32, x.shape, 1)
    return jnp.where((lane // size) % 2 == 0, pltpu.roll(x, lanes - size, 1), pltpu.roll(x, size, 1))


def logit_grad_kernel(place, n_stats, tile, ids, *refs):
    stats = refs[:n_stats]
    teachers = refs[n_stats : n_stats + place.nv]
    e_ref, g_ref, cols_sc = refs[n_stats + place.nv :]
    rows = g_ref.shape[0]
    half = rows // 2
    me = ids[0] * place.nv + ids[1]

    tops, totals, teacher = [], [], []
    for zk, ref in enumerate(stats):
        for ck in range(2):
            x = ref[8 * ck : 8 * ck + 8, :]
            teacher.append(x[2:4, : rows // place.nv])
            if ck:
                x = jnp.concatenate([x[:, half:], x[:, :half]], axis=1)
            bit = 1
            while bit < place.nz:
                if zk & bit:
                    x = swap_groups(x, bit * place.group, rows)
                bit *= 2
            tops.append(x[0:1])
            totals.append(x[1:2])
    top = functools.reduce(jnp.maximum, tops)
    total = sum(t * jnp.exp(m - top) for m, t in zip(tops, totals))
    scale = jnp.exp(tops[0] - top) / total
    teacher = jnp.concatenate(teacher, axis=1)
    packed = jnp.concatenate(
        [scale, teacher[0:1], 1.0 / teacher[1:2], jnp.zeros((LANES - 3, rows), F32)], axis=0
    )
    cols_sc[...] = packed.T

    @pl.loop(0, g_ref.shape[1] // tile)
    def _(j):
        across = pl.ds(pl.multiple_of(j * tile, tile), tile)
        for i, t_ref in enumerate(teachers):
            step, ck = divmod(i, 2)
            per = t_ref.shape[0] // place.group
            source = ids[2 + step] * 2 + jnp.bitwise_xor(jnp.bitwise_and(ids[1], 1), ck)
            vk = jnp.bitwise_xor(source, ids[1])
            for sub in range(per):
                can = source * per + sub
                to = place.position(jnp.bitwise_xor(me, can)) * place.group
                to = pl.ds(pl.multiple_of(to, place.group), place.group)
                c = cols_sc[to, :]
                at = pl.multiple_of((vk * per + sub) * place.group, place.group)
                d = cols_sc[pl.ds(at, place.group), :]
                t = t_ref[sub * place.group : (sub + 1) * place.group, across].astype(F32)
                q = jnp.exp(t - d[:, 1:2]) * d[:, 2:3]
                g_ref[to, across] = (e_ref[to, across] * c[:, 0:1] - q).astype(BF16)


def logit_grad(place, ids, stats, teachers, e, tile):
    rows, cols = e.shape
    return pl.pallas_call(
        functools.partial(logit_grad_kernel, place, len(stats), tile),
        in_specs=[pl.BlockSpec(memory_space=pltpu.SMEM)]
        + [WHOLE] * (len(stats) + len(teachers) + 1),
        out_specs=WHOLE,
        out_shape=jax.ShapeDtypeStruct((rows, cols), BF16),
        scratch_shapes=[pltpu.VMEM((rows, LANES), F32)],
        compiler_params=params(8 * rows * cols + 4 * LANES * rows),
        cost_estimate=cost(8 * rows * cols, 8 * rows * cols),
        name="logit_grad",
    )(ids, *stats, *teachers, e)


def input_grad_kernel(start, tile, g_ref, w_ref, keep_ref, send_ref):
    half = g_ref.shape[0] // 2

    @pl.loop(0, keep_ref.shape[1] // tile)
    def _(j):
        at = pl.ds(pl.multiple_of(j * tile, tile), tile)
        w = w_ref[pl.ds(pl.multiple_of(start + j * tile, tile), tile), :]
        out = lax.dot_general(g_ref[...], w, NT, preferred_element_type=F32)
        keep_ref[:, at] = out[:half]
        send_ref[:, at] = out[half:].astype(BF16)


def input_grad_part(g, weight, start, width, tile):
    rows, cols = g.shape
    return pl.pallas_call(
        functools.partial(input_grad_kernel, start, tile),
        in_specs=[WHOLE] * 2,
        out_specs=[WHOLE] * 2,
        out_shape=[
            jax.ShapeDtypeStruct((rows // 2, width), F32),
            jax.ShapeDtypeStruct((rows // 2, width), BF16),
        ],
        compiler_params=params(2 * rows * cols + 2 * weight.size + 3 * rows * width),
        cost_estimate=cost(2 * rows * cols * width, 2 * cols * (rows + width)),
        name="input_grad",
    )(g, weight)


def weight_grad_kernel(h_ref, g_ref, *refs):
    o_ref = refs[-1]
    o_ref[0] = lax.dot_general(h_ref[...], g_ref[...], TN, preferred_element_type=F32).astype(BF16)


def weight_grad_part(h, g, before, part, parts, tile):
    rows, depth = h.shape
    cols = g.shape[1]
    steps = cols // parts // tile
    start = part * steps
    extra = [] if before is None else [before]
    return pl.pallas_call(
        weight_grad_kernel,
        grid=(steps,),
        in_specs=[
            pl.BlockSpec((rows, depth), lambda j: (0, 0)),
            pl.BlockSpec((rows, tile), lambda j: (0, start + j)),
        ]
        + [pl.BlockSpec(memory_space=pl.ANY)] * len(extra),
        out_specs=pl.BlockSpec((1, depth, tile), lambda j: (0, 0, start + j)),
        out_shape=jax.ShapeDtypeStruct((1, depth, cols), BF16),
        input_output_aliases={2: 0} if extra else {},
        compiler_params=params(4 * depth * rows + 4 * rows * tile + 8 * depth * tile),
        cost_estimate=cost(2 * rows * cols * depth // parts, 2 * depth * cols // parts),
        name="weight_grad",
    )(h, g, *extra)


class Place:
    def __init__(self, nh, nv, group):
        self.nh, self.nv, self.nz, self.group = nh, nv, nv // 2, group

    def bits(self, r):
        ck, rest = divmod(r, self.nh * self.nz)
        hk, zk = divmod(rest, self.nz)
        return hk * self.nv + zk * 2 + ck

    def position(self, d):
        hk, vk = d // self.nv, d % self.nv
        zk, ck = vk // 2, vk % 2
        return (ck * self.nh + hk) * self.nz + zk


def swap(x, axis, size, k):
    return lax.ppermute(x, axis, [(i, i ^ k) for i in range(size)])


def coded(i):
    return i ^ (i >> 1)


def shifted(z, nz, step):
    place, rest = z, z >> 1
    bits = nz
    while bits > 2:
        place, rest, bits = place ^ rest, rest >> 1, bits // 2
    return coded((place + step) % nz)


def relative(nh, nv, hidden, weight, teacher):
    place = Place(nh, nv, hidden.shape[0])
    nz = place.nz
    v = lax.axis_index("vocab")
    z, core = v // 2, v % 2
    sources = [shifted(z, nz, nz - step) for step in range(nz)]
    ids = jnp.stack([lax.axis_index("head"), v] + sources).astype(jnp.int32)
    cols = weight.shape[2]

    near = [hidden] + [None] * (nz - 1)
    for k in range(nz - 1, 0, -1):
        near[k] = swap(hidden, "vocab", nv, 2 * k)

    def piece(step, ck):
        to = shifted(z, nz, step) * 2 + (core ^ ck)
        return lax.dynamic_slice(teacher, (0, 0, to * cols), (1, teacher.shape[1], cols))[0]

    def move(x, step):
        pairs = [(2 * i + c, 2 * shifted(i, nz, step) + c) for i in range(nz) for c in range(2)]
        return lax.ppermute(x, "vocab", pairs)

    blocks = []
    pieces = lax.optimization_barrier(
        tuple((piece(step, 0), piece(step, 1)) for step in range(nz))
    )
    for step in range(nz):
        mine, cross = pieces[step]
        cross = swap(cross, "vocab", nv, 1)
        if step:
            mine = move(mine, step)
            cross = move(cross, step)
        blocks += [mine, cross]

    block = stacked(near)
    own = [block]
    for k in range(1, nh):
        own.append(swap(block, "head", nh, k))
    other = []
    for k in range(nh):
        other.append(swap(own[k], "vocab", nv, 1))

    e, h, stat = student(own + other, weight[0], teacher_stats(teacher), 512)
    pair = swap(stat, "vocab", nv, 1)
    pair = stacked([stat, pair])
    stats = [pair]
    for k in range(1, nz):
        stats.append(swap(pair, "vocab", nv, 2 * k))
    g = logit_grad(place, ids, stats, blocks, e, 1024)

    depth = weight.shape[1]
    chunks = 2
    width = depth // chunks
    rows = place.group * nz
    sums = []
    for c in range(chunks):
        keep, send = input_grad_part(g, weight[0], c * width, width, 512)
        send = swap(send, "vocab", nv, 1)
        keep = keep + send.astype(F32)
        part = [keep[k * rows : (k + 1) * rows] for k in range(nh)]
        total = part[0]
        for k in range(1, nh):
            part[k] = swap(part[k].astype(BF16), "head", nh, k)
            total = total + part[k].astype(F32)
        part = [total[k * place.group : (k + 1) * place.group] for k in range(nz)]
        total = part[0]
        for k in range(1, nz):
            part[k] = swap(part[k].astype(BF16), "vocab", nv, 2 * k)
            total = total + part[k].astype(F32)
        sums.append(total)
    grad = None
    for part in range(PARTS):
        grad = weight_grad_part(h, g, grad, part, PARTS, 512)
    return (grad, jnp.concatenate(sums, axis=1))


PARTS = 4


def gathered(hidden, weight, teacher):
    trunk = lax.all_gather(hidden, ("head", "vocab"), axis=0, tiled=True)
    weight = weight[0]
    teacher = lax.all_to_all(teacher, "vocab", split_axis=2, concat_axis=1, tiled=True)[0]
    teacher = teacher.astype(F32)
    s = jnp.dot(trunk, weight, preferred_element_type=F32)
    tops = [jnp.max(x, axis=1) for x in (s, teacher)]
    totals = [jnp.sum(jnp.exp(x - m[:, None]), axis=1) for x, m in zip((s, teacher), tops)]
    stat = lax.all_gather(jnp.stack(tops + totals), "vocab")
    prob = []
    for i, x in enumerate((s, teacher)):
        top = jnp.max(stat[:, i], axis=0)
        total = jnp.sum(stat[:, i + 2] * jnp.exp(stat[:, i] - top), axis=0)
        prob.append(jnp.exp(x - top[:, None]) / total[:, None])
    g = (prob[0] - prob[1]).astype(BF16)
    grad = lax.dot_general(trunk, g, TN, preferred_element_type=F32).astype(BF16)[None]
    back = lax.dot_general(g, weight, NT, preferred_element_type=F32)
    return (grad, lax.psum_scatter(back, ("head", "vocab"), scatter_dimension=0, tiled=True))


def per_device(nh, nv, plain, hidden, weight, teacher):
    if plain:
        return gathered(hidden, weight, teacher)
    return relative(nh, nv, hidden, weight, teacher)


def solution(mesh):
    nh, nv = mesh.shape["head"], mesh.shape["vocab"]

    def step(hidden, weight, teacher):
        group = hidden.shape[0] // (nh * nv)
        plain = nh & (nh - 1) or nv & (nv - 1) or group % 16
        run = jax.shard_map(
            functools.partial(per_device, nh, nv, plain),
            mesh=mesh,
            in_specs=(P(("head", "vocab"), None), P("head", None, "vocab"), P("head", "vocab", None)),
            out_specs=(P("head", None, "vocab"), P(("head", "vocab"), None)),
            check_vma=False,
        )
        return run(hidden, weight, teacher)

    return step
```

```python
import functools

import jax
import jax.numpy as jnp
from jax import lax
from jax.experimental import pallas as pl
from jax.experimental.pallas import tpu as pltpu
from jax.sharding import PartitionSpec as P


F32 = jnp.float32
BF16 = jnp.bfloat16
LANES = 128
NT = (((1,), (1,)), ((), ()))
TN = (((0,), (0,)), ((), ()))
MIB = 1024 * 1024


def params(nbytes):
    return pltpu.CompilerParams(vmem_limit_bytes=nbytes + 4 * MIB)


def cost(flops, nbytes):
    return pl.CostEstimate(flops=flops, bytes_accessed=nbytes, transcendentals=0)


WHOLE = pl.BlockSpec(memory_space=pltpu.VMEM)


def teacher_stats_kernel(t_hbm, o_ref, x_ref, cols_sc, sem):
    copy = pltpu.make_async_copy(t_hbm.at[0], x_ref, sem)
    copy.start()
    rows, cols = x_ref.shape
    cols_sc[...] = jnp.zeros_like(cols_sc)
    step = 16
    lane = lax.broadcasted_iota(jnp.int32, (step, LANES), 1)
    copy.wait()
    for at in range(0, rows, step):
        pieces = [slice(c, c + LANES) for c in range(0, cols, LANES)]
        top = [jnp.full((step, LANES), -jnp.inf, F32)] * 4
        for i, c in enumerate(pieces):
            top[i % 4] = jnp.maximum(top[i % 4], x_ref[at : at + step, c].astype(F32))
        top = functools.reduce(jnp.maximum, top)
        top = jnp.max(top, axis=1, keepdims=True)
        wide = jnp.broadcast_to(top, (step, LANES))
        total = [jnp.zeros((step, LANES), F32)] * 4
        for i, c in enumerate(pieces):
            total[i % 4] = total[i % 4] + jnp.exp(x_ref[at : at + step, c].astype(F32) - wide)
        total = jnp.sum(sum(total), axis=1, keepdims=True)
        cols_sc[at : at + step, :] = jnp.where(lane == 0, wide, jnp.where(lane == 1, total, 0.0))
    o_ref[...] = cols_sc[...].T[:8, :]


def teacher_stats(teacher):
    _, rows, cols = teacher.shape
    return pl.pallas_call(
        teacher_stats_kernel,
        in_specs=[pl.BlockSpec(memory_space=pl.ANY)],
        out_specs=WHOLE,
        out_shape=jax.ShapeDtypeStruct((8, LANES), F32),
        scratch_shapes=[
            pltpu.VMEM((rows, cols), BF16),
            pltpu.VMEM((LANES, LANES), F32),
            pltpu.SemaphoreType.DMA,
        ],
        compiler_params=params(2 * rows * cols + 4 * LANES * LANES),
        cost_estimate=cost(8 * rows * cols, 2 * rows * cols),
        name="teacher_stats",
    )(teacher)


def stack_kernel(*refs):
    rows = refs[0].shape[0]
    for i, ref in enumerate(refs[:-1]):
        refs[-1][i * rows : (i + 1) * rows, :] = ref[...]


def stacked(parts):
    rows, cols = parts[0].shape
    shape = jax.ShapeDtypeStruct((rows * len(parts), cols), parts[0].dtype)
    nbytes = shape.size * shape.dtype.itemsize
    return pl.pallas_call(
        stack_kernel,
        in_specs=[WHOLE] * len(parts),
        out_specs=WHOLE,
        out_shape=shape,
        compiler_params=params(0),
        cost_estimate=cost(0, 2 * nbytes),
    )(*parts)


def student_kernel(pieces, tile, own, *refs):
    parts, (w_ref, t_ref, e_ref, h_ref, stat_ref, s_ref, cols_sc) = refs[:pieces], refs[pieces:]
    rows = parts[0].shape[0]
    for i, part in enumerate(parts):
        h_ref[i * rows : (i + 1) * rows, :] = part[...]
    for at in range(0, w_ref.shape[1], tile):
        w = w_ref[:, at : at + tile]
        s_ref[:, at : at + tile] = jnp.dot(h_ref[...], w, preferred_element_type=F32)

    step = 8
    lane = lax.broadcasted_iota(jnp.int32, (step, LANES), 1)

    def body(i, _):
        at = pl.ds(pl.multiple_of(i * step, step), step)
        x = s_ref[at, :]
        top = jnp.max(x, axis=1, keepdims=True)
        e = jnp.exp(x - top)
        e_ref[at, :] = e
        total = jnp.sum(e, axis=1, keepdims=True)
        cols_sc[at, :] = jnp.where(lane == 0, top, jnp.where(lane == 1, total, 0.0))
        return _

    lax.fori_loop(0, e_ref.shape[0] // step, body, 0, unroll=8)
    stat_ref[...] = cols_sc[...].T[:8, :]
    stat_ref[2:4, :own] = t_ref[:2, :own]


def student(parts, weight, tstat, own, tile):
    depth, cols = weight.shape
    rows = sum(p.shape[0] for p in parts)
    return pl.pallas_call(
        functools.partial(student_kernel, len(parts), tile, own),
        in_specs=[WHOLE] * (len(parts) + 2),
        out_specs=[WHOLE] * 3,
        out_shape=[
            jax.ShapeDtypeStruct((rows, cols), F32),
            jax.ShapeDtypeStruct((rows, depth), BF16),
            jax.ShapeDtypeStruct((8, rows), F32),
        ],
        scratch_shapes=[pltpu.VMEM((rows, cols), F32), pltpu.VMEM((rows, LANES), F32)],
        compiler_params=params(4 * rows * (cols + LANES)),
        cost_estimate=cost(2 * rows * cols * depth, 2 * depth * cols + 4 * rows * cols),
        name="student",
    )(*parts, weight, tstat)


def swap_groups(x, size, lanes):
    lane = lax.broadcasted_iota(jnp.int32, x.shape, 1)
    return jnp.where((lane // size) % 2 == 0, pltpu.roll(x, lanes - size, 1), pltpu.roll(x, size, 1))


def logit_grad_kernel(place, n_stats, tile, *refs):
    stats = refs[:n_stats]
    teachers = refs[n_stats : n_stats + place.nv]
    e_ref, g_ref, cols_sc = refs[n_stats + place.nv :]
    rows = g_ref.shape[0]
    half = rows // 2
    v = lax.axis_index("vocab")
    me = lax.axis_index("head") * place.nv + v

    tops, totals, teacher = [], [], []
    for zk, ref in enumerate(stats):
        for ck in range(2):
            x = ref[8 * ck : 8 * ck + 8, :]
            teacher.append(x[2:4, : rows // place.nv])
            if ck:
                x = jnp.concatenate([x[:, half:], x[:, :half]], axis=1)
            bit = 1
            while bit < place.nz:
                if zk & bit:
                    x = swap_groups(x, bit * place.group, rows)
                bit *= 2
            tops.append(x[0:1])
            totals.append(x[1:2])
    top = functools.reduce(jnp.maximum, tops)
    total = sum(t * jnp.exp(m - top) for m, t in zip(tops, totals))
    scale = jnp.exp(tops[0] - top) / total
    teacher = jnp.concatenate(teacher, axis=1)
    packed = jnp.concatenate(
        [scale, teacher[0:1], 1.0 / teacher[1:2], jnp.zeros((LANES - 3, rows), F32)], axis=0
    )
    cols_sc[...] = packed.T

    @pl.loop(0, g_ref.shape[1] // tile)
    def _(j):
        across = pl.ds(pl.multiple_of(j * tile, tile), tile)
        for i, t_ref in enumerate(teachers):
            step, ck = divmod(i, 2)
            per = t_ref.shape[0] // place.group
            source = shifted(v >> 1, place.nz, place.nz - step) * 2 + jnp.bitwise_xor(v & 1, ck)
            vk = jnp.bitwise_xor(source, v)
            for sub in range(per):
                can = source * per + sub
                to = place.position(jnp.bitwise_xor(me, can)) * place.group
                to = pl.ds(pl.multiple_of(to, place.group), place.group)
                c = cols_sc[to, :]
                at = pl.multiple_of((vk * per + sub) * place.group, place.group)
                d = cols_sc[pl.ds(at, place.group), :]
                t = t_ref[sub * place.group : (sub + 1) * place.group, across].astype(F32)
                q = jnp.exp(t - d[:, 1:2]) * d[:, 2:3]
                g_ref[to, across] = (e_ref[to, across] * c[:, 0:1] - q).astype(BF16)


def logit_grad(place, stats, teachers, e, tile):
    rows, cols = e.shape
    return pl.pallas_call(
        functools.partial(logit_grad_kernel, place, len(stats), tile),
        in_specs=[WHOLE] * (len(stats) + len(teachers) + 1),
        out_specs=WHOLE,
        out_shape=jax.ShapeDtypeStruct((rows, cols), BF16),
        scratch_shapes=[pltpu.VMEM((rows, LANES), F32)],
        compiler_params=params(4 * rows * LANES),
        cost_estimate=cost(8 * rows * cols, 8 * rows * cols),
        name="logit_grad",
    )(*stats, *teachers, e)


def input_grad_kernel(start, tile, g_ref, w_ref, keep_ref, send_ref):
    half = g_ref.shape[0] // 2

    @pl.loop(0, keep_ref.shape[1] // tile)
    def _(j):
        at = pl.ds(pl.multiple_of(j * tile, tile), tile)
        w = w_ref[pl.ds(pl.multiple_of(start + j * tile, tile), tile), :]
        out = lax.dot_general(g_ref[...], w, NT, preferred_element_type=F32)
        keep_ref[:, at] = out[:half]
        send_ref[:, at] = out[half:].astype(BF16)


def input_grad_part(g, weight, start, width, tile):
    rows, cols = g.shape
    return pl.pallas_call(
        functools.partial(input_grad_kernel, start, tile),
        in_specs=[WHOLE] * 2,
        out_specs=[WHOLE] * 2,
        out_shape=[
            jax.ShapeDtypeStruct((rows // 2, width), F32),
            jax.ShapeDtypeStruct((rows // 2, width), BF16),
        ],
        compiler_params=params(4 * rows * tile),
        cost_estimate=cost(2 * rows * cols * width, 2 * cols * (rows + width)),
        name="input_grad",
    )(g, weight)


def turn_kernel(h_ref, w_hbm, o_ref, w_ref, sem):
    copy = pltpu.make_async_copy(w_hbm, w_ref, sem)
    copy.start()
    o_ref[...] = h_ref[...].T
    copy.wait()


def turned(h, weight):
    rows, depth = h.shape
    return pl.pallas_call(
        turn_kernel,
        in_specs=[WHOLE, pl.BlockSpec(memory_space=pl.ANY)],
        out_specs=[WHOLE] * 2,
        out_shape=[
            jax.ShapeDtypeStruct((depth, rows), BF16),
            jax.ShapeDtypeStruct(weight.shape, BF16),
        ],
        scratch_shapes=[pltpu.SemaphoreType.DMA],
        compiler_params=params(0),
        cost_estimate=cost(0, 4 * rows * depth + 4 * weight.size),
        name="turn",
    )(h, weight)


def weight_grad_kernel(start, tile, ht_ref, g_ref, *refs):
    at = pl.multiple_of((start + pl.program_id(0)) * tile, tile)
    g = g_ref[:, pl.ds(at, tile)]
    refs[-1][0] = jnp.dot(ht_ref[...], g, preferred_element_type=F32).astype(BF16)


def weight_grad_part(ht, g, before, part, parts, tile):
    depth, rows = ht.shape
    cols = g.shape[1]
    steps = cols // parts // tile
    start = part * steps
    extra = [] if before is None else [before]
    return pl.pallas_call(
        functools.partial(weight_grad_kernel, start, tile),
        grid=(steps,),
        in_specs=[WHOLE] * 2 + [pl.BlockSpec(memory_space=pl.ANY)] * len(extra),
        out_specs=pl.BlockSpec((1, depth, tile), lambda j: (0, 0, start + j)),
        out_shape=jax.ShapeDtypeStruct((1, depth, cols), BF16),
        input_output_aliases={2: 0} if extra else {},
        compiler_params=params(8 * depth * tile),
        cost_estimate=cost(2 * rows * cols * depth // parts, 2 * depth * cols // parts),
        name="weight_grad",
    )(ht, g, *extra)


class Place:
    def __init__(self, nh, nv, group):
        self.nh, self.nv, self.nz, self.group = nh, nv, nv // 2, group

    def bits(self, r):
        ck, rest = divmod(r, self.nh * self.nz)
        hk, zk = divmod(rest, self.nz)
        return hk * self.nv + zk * 2 + ck

    def position(self, d):
        hk, vk = d // self.nv, d % self.nv
        zk, ck = vk // 2, vk % 2
        return (ck * self.nh + hk) * self.nz + zk


def swap(x, axis, size, k):
    return lax.ppermute(x, axis, [(i, i ^ k) for i in range(size)])


def coded(i):
    return i ^ (i >> 1)


def shifted(z, nz, step):
    place, rest = z, z >> 1
    bits = nz
    while bits > 2:
        place, rest, bits = place ^ rest, rest >> 1, bits // 2
    return coded((place + step) & (nz - 1))


def relative(nh, nv, hidden, weight, teacher):
    place = Place(nh, nv, hidden.shape[0])
    nz = place.nz
    v = lax.axis_index("vocab")
    z, core = v >> 1, v & 1
    cols = weight.shape[2]

    near = [hidden] + [None] * (nz - 1)
    for k in range(nz - 1, 0, -1):
        near[k] = swap(hidden, "vocab", nv, 2 * k)

    def piece(step, ck):
        to = shifted(z, nz, step) * 2 + (core ^ ck)
        return lax.dynamic_slice(teacher, (0, 0, to * cols), (1, teacher.shape[1], cols))[0]

    def move(x, step, ck):
        pairs = [
            (2 * i + c, 2 * shifted(i, nz, step) + (c ^ ck)) for i in range(nz) for c in range(2)
        ]
        return lax.ppermute(x, "vocab", pairs)

    blocks = []
    pieces = lax.optimization_barrier(
        tuple((piece(step, 0), piece(step, 1)) for step in range(nz))
    )
    for step in range(nz):
        mine, cross = pieces[step]
        if step:
            mine = move(mine, step, 0)
        cross = move(cross, step, 1)
        blocks += [mine, cross]

    block = stacked(near)
    own = [block]
    for k in range(1, nh):
        own.append(swap(block, "head", nh, k))
    other = []
    for k in range(nh):
        other.append(swap(own[k], "vocab", nv, 1))

    tstat = teacher_stats(teacher)
    e, h, stat = student(own + other, weight[0], tstat, teacher.shape[1], 512)
    pair = swap(stat, "vocab", nv, 1)
    pair = stacked([stat, pair])
    stats = [pair]
    for k in range(1, nz):
        stats.append(swap(pair, "vocab", nv, 2 * k))
    ht, near_weight = turned(h, weight[0])
    g = logit_grad(place, stats, blocks, e, 1024)

    depth = weight.shape[1]
    chunks = 2
    width = depth // chunks
    rows = place.group * nz
    keeps, sums = [], []
    for c in range(chunks):
        keep, send = input_grad_part(g, near_weight, c * width, width, 512)
        send = swap(send, "vocab", nv, 1)
        keeps.append(keep + send.astype(F32))
    for keep in keeps:
        part = [keep[k * rows : (k + 1) * rows] for k in range(nh)]
        total = part[0]
        for k in range(1, nh):
            part[k] = swap(part[k].astype(BF16), "head", nh, k)
            total = total + part[k].astype(F32)
        sums.append(total)
    total = jnp.concatenate(sums, axis=1)
    part = [total[k * place.group : (k + 1) * place.group] for k in range(nz)]
    total = part[0]
    for k in range(1, nz):
        part[k] = swap(part[k].astype(BF16), "vocab", nv, 2 * k)
        total = total + part[k].astype(F32)
    grad = None
    for part in range(PARTS):
        grad = weight_grad_part(ht, g, grad, part, PARTS, 256)
    return (grad, total)


PARTS = 4


def gathered(hidden, weight, teacher):
    trunk = lax.all_gather(hidden, ("head", "vocab"), axis=0, tiled=True)
    weight = weight[0]
    teacher = lax.all_to_all(teacher, "vocab", split_axis=2, concat_axis=1, tiled=True)[0]
    teacher = teacher.astype(F32)
    s = jnp.dot(trunk, weight, preferred_element_type=F32)
    tops = [jnp.max(x, axis=1) for x in (s, teacher)]
    totals = [jnp.sum(jnp.exp(x - m[:, None]), axis=1) for x, m in zip((s, teacher), tops)]
    stat = lax.all_gather(jnp.stack(tops + totals), "vocab")
    prob = []
    for i, x in enumerate((s, teacher)):
        top = jnp.max(stat[:, i], axis=0)
        total = jnp.sum(stat[:, i + 2] * jnp.exp(stat[:, i] - top), axis=0)
        prob.append(jnp.exp(x - top[:, None]) / total[:, None])
    g = (prob[0] - prob[1]).astype(BF16)
    grad = lax.dot_general(trunk, g, TN, preferred_element_type=F32).astype(BF16)[None]
    back = lax.dot_general(g, weight, NT, preferred_element_type=F32)
    return (grad, lax.psum_scatter(back, ("head", "vocab"), scatter_dimension=0, tiled=True))


def per_device(nh, nv, plain, hidden, weight, teacher):
    if plain:
        return gathered(hidden, weight, teacher)
    return relative(nh, nv, hidden, weight, teacher)


def solution(mesh):
    nh, nv = mesh.shape["head"], mesh.shape["vocab"]

    def step(hidden, weight, teacher):
        group = hidden.shape[0] // (nh * nv)
        plain = nh & (nh - 1) or nv & (nv - 1) or group % 16
        run = jax.shard_map(
            functools.partial(per_device, nh, nv, plain),
            mesh=mesh,
            in_specs=(P(("head", "vocab"), None), P("head", None, "vocab"), P("head", "vocab", None)),
            out_specs=(P("head", None, "vocab"), P(("head", "vocab"), None)),
            check_vma=False,
        )
        return run(hidden, weight, teacher)

    return step
```

```python
import functools

import jax
import jax.numpy as jnp
from jax import lax
from jax.experimental import pallas as pl
from jax.experimental.pallas import tpu as pltpu
from jax.sharding import PartitionSpec as P


F32 = jnp.float32
BF16 = jnp.bfloat16
LANES = 128
NT = (((1,), (1,)), ((), ()))
TN = (((0,), (0,)), ((), ()))
MIB = 1024 * 1024
ROOM = 42 * MIB


def params(nbytes):
    return pltpu.CompilerParams(vmem_limit_bytes=nbytes + 4 * MIB)


def cost(flops, nbytes):
    return pl.CostEstimate(flops=flops, bytes_accessed=nbytes, transcendentals=0)


WHOLE = pl.BlockSpec(memory_space=pltpu.VMEM)
STORED = pl.BlockSpec(memory_space=pltpu.HBM)


def prepare_kernel(t_hbm, w_hbm, o_ref, w_ref, x_ref, cols_sc, sem):
    copy = pltpu.make_async_copy(t_hbm.at[0], x_ref, sem.at[0])
    copy.start()
    weight = pltpu.make_async_copy(w_hbm, w_ref, sem.at[1])
    weight.start()
    rows, cols = x_ref.shape
    cols_sc[...] = jnp.zeros_like(cols_sc)
    step = 16
    lane = lax.broadcasted_iota(jnp.int32, (step, LANES), 1)
    copy.wait()
    for at in range(0, rows, step):
        pieces = [slice(c, c + LANES) for c in range(0, cols, LANES)]
        top = [jnp.full((step, LANES), -jnp.inf, F32)] * 4
        for i, c in enumerate(pieces):
            top[i % 4] = jnp.maximum(top[i % 4], x_ref[at : at + step, c].astype(F32))
        top = functools.reduce(jnp.maximum, top)
        top = jnp.max(top, axis=1, keepdims=True)
        wide = jnp.broadcast_to(top, (step, LANES))
        total = [jnp.zeros((step, LANES), F32)] * 4
        for i, c in enumerate(pieces):
            total[i % 4] = total[i % 4] + jnp.exp(x_ref[at : at + step, c].astype(F32) - wide)
        total = jnp.sum(sum(total), axis=1, keepdims=True)
        cols_sc[at : at + step, :] = jnp.where(lane == 0, wide, jnp.where(lane == 1, total, 0.0))
    o_ref[...] = cols_sc[...].T[:8, :]
    weight.wait()


def prepared(teacher, weight):
    _, rows, cols = teacher.shape
    return pl.pallas_call(
        prepare_kernel,
        in_specs=[STORED] * 2,
        out_specs=[WHOLE] * 2,
        out_shape=[
            jax.ShapeDtypeStruct((8, LANES), F32),
            jax.ShapeDtypeStruct(weight.shape, BF16),
        ],
        scratch_shapes=[
            pltpu.VMEM((rows, cols), BF16),
            pltpu.VMEM((LANES, LANES), F32),
            pltpu.SemaphoreType.DMA((2,)),
        ],
        compiler_params=pltpu.CompilerParams(vmem_limit_bytes=ROOM),
        cost_estimate=cost(8 * rows * cols, 2 * rows * cols + 4 * weight.size),
        name="prepare",
    )(teacher, weight)


def stack_kernel(*refs):
    rows = refs[0].shape[0]
    for i, ref in enumerate(refs[:-1]):
        refs[-1][i * rows : (i + 1) * rows, :] = ref[...]


def stacked(parts):
    rows, cols = parts[0].shape
    shape = jax.ShapeDtypeStruct((rows * len(parts), cols), parts[0].dtype)
    nbytes = shape.size * shape.dtype.itemsize
    return pl.pallas_call(
        stack_kernel,
        in_specs=[WHOLE] * len(parts),
        out_specs=WHOLE,
        out_shape=shape,
        compiler_params=params(0),
        cost_estimate=cost(0, 2 * nbytes),
    )(*parts)


def student_kernel(pieces, tile, own, *refs):
    parts, (w_ref, t_ref, e_ref, h_ref, stat_ref, s_ref, cols_sc) = refs[:pieces], refs[pieces:]
    rows = parts[0].shape[0]
    for i, part in enumerate(parts):
        h_ref[i * rows : (i + 1) * rows, :] = part[...]
    for at in range(0, w_ref.shape[1], tile):
        w = w_ref[:, at : at + tile]
        s_ref[:, at : at + tile] = jnp.dot(h_ref[...], w, preferred_element_type=F32)

    step = 8
    lane = lax.broadcasted_iota(jnp.int32, (step, LANES), 1)

    def body(i, _):
        at = pl.ds(pl.multiple_of(i * step, step), step)
        x = s_ref[at, :]
        top = jnp.max(x, axis=1, keepdims=True)
        e = jnp.exp(x - top)
        e_ref[at, :] = e
        total = jnp.sum(e, axis=1, keepdims=True)
        cols_sc[at, :] = jnp.where(lane == 0, top, jnp.where(lane == 1, total, 0.0))
        return _

    lax.fori_loop(0, e_ref.shape[0] // step, body, 0, unroll=8)
    stat_ref[...] = cols_sc[...].T[:8, :]
    stat_ref[2:4, :own] = t_ref[:2, :own]


def student(parts, weight, tstat, own, tile):
    depth, cols = weight.shape
    rows = sum(p.shape[0] for p in parts)
    return pl.pallas_call(
        functools.partial(student_kernel, len(parts), tile, own),
        in_specs=[WHOLE] * (len(parts) + 2),
        out_specs=[WHOLE] * 3,
        out_shape=[
            jax.ShapeDtypeStruct((rows, cols), F32),
            jax.ShapeDtypeStruct((rows, depth), BF16),
            jax.ShapeDtypeStruct((8, rows), F32),
        ],
        scratch_shapes=[pltpu.VMEM((rows, cols), F32), pltpu.VMEM((rows, LANES), F32)],
        compiler_params=params(4 * rows * (cols + LANES)),
        cost_estimate=cost(2 * rows * cols * depth, 2 * depth * cols + 4 * rows * cols),
        name="student",
    )(*parts, weight, tstat)


def swap_groups(x, size, lanes):
    lane = lax.broadcasted_iota(jnp.int32, x.shape, 1)
    return jnp.where((lane // size) % 2 == 0, pltpu.roll(x, lanes - size, 1), pltpu.roll(x, size, 1))


def logit_grad_kernel(place, part, n_stats, tile, *refs):
    stats = refs[:n_stats]
    teachers = refs[n_stats : n_stats + place.nv]
    e_ref, *before, g_ref, cols_sc = refs[n_stats + place.nv :]
    rows = e_ref.shape[0]
    half = rows // 2
    if part:
        g_ref[:half, :] = before[0][...]
    v = lax.axis_index("vocab")
    me = lax.axis_index("head") * place.nv + v

    tops, totals, teacher = [], [], []
    for zk, ref in enumerate(stats):
        for ck in range(2):
            x = ref[8 * ck : 8 * ck + 8, :]
            teacher.append(x[2:4, : rows // place.nv])
            if ck:
                x = jnp.concatenate([x[:, half:], x[:, :half]], axis=1)
            bit = 1
            while bit < place.nz:
                if zk & bit:
                    x = swap_groups(x, bit * place.group, rows)
                bit *= 2
            tops.append(x[0:1])
            totals.append(x[1:2])
    top = functools.reduce(jnp.maximum, tops)
    total = sum(t * jnp.exp(m - top) for m, t in zip(tops, totals))
    scale = jnp.exp(tops[0] - top) / total
    teacher = jnp.concatenate(teacher, axis=1)
    packed = jnp.concatenate(
        [scale, teacher[0:1], 1.0 / teacher[1:2], jnp.zeros((LANES - 3, rows), F32)], axis=0
    )
    cols_sc[...] = packed.T

    @pl.loop(0, g_ref.shape[1] // tile)
    def _(j):
        across = pl.ds(pl.multiple_of(j * tile, tile), tile)
        for i, t_ref in enumerate(teachers):
            step, ck = divmod(i, 2)
            per = t_ref.shape[0] // place.group
            source = shifted(v >> 1, place.nz, place.nz - step) * 2 + jnp.bitwise_xor(v & 1, ck)
            vk = jnp.bitwise_xor(source, v)
            for sub in range(per):
                can = (source * 2 + part) * per + sub
                d = jnp.bitwise_xor(me, can)
                at = pl.multiple_of(place.position(d) * place.group, place.group)
                at = pl.ds(at, place.group)
                to = pl.multiple_of(place.half_position(d) * place.group, place.group)
                to = pl.ds(part * half + to, place.group)
                c = cols_sc[at, :]
                own = pl.multiple_of(((vk * 2 + part) * per + sub) * place.group, place.group)
                own = cols_sc[pl.ds(own, place.group), :]
                t = t_ref[sub * place.group : (sub + 1) * place.group, across].astype(F32)
                q = jnp.exp(t - own[:, 1:2]) * own[:, 2:3]
                g_ref[to, across] = (e_ref[at, across] * c[:, 0:1] - q).astype(BF16)


def logit_grad(place, part, stats, teachers, e, before, tile):
    rows, cols = e.shape
    if not part:
        rows //= 2
    return pl.pallas_call(
        functools.partial(logit_grad_kernel, place, part, len(stats), tile),
        in_specs=[WHOLE] * (len(stats) + len(teachers) + 1 + len(before)),
        out_specs=WHOLE,
        out_shape=jax.ShapeDtypeStruct((rows, cols), BF16),
        scratch_shapes=[pltpu.VMEM((e.shape[0], LANES), F32)],
        compiler_params=params(4 * e.shape[0] * LANES),
        cost_estimate=cost(8 * rows * cols, 8 * rows * cols),
        name="logit_grad",
    )(*stats, *teachers, e, *before)


def input_grad_kernel(start, tile, g_ref, w_ref, keep_ref, send_ref):
    half = keep_ref.shape[0]
    g = g_ref.at[start : start + 2 * half]

    @pl.loop(0, keep_ref.shape[1] // tile)
    def _(j):
        at = pl.ds(pl.multiple_of(j * tile, tile), tile)
        out = lax.dot_general(g[...], w_ref[at, :], NT, preferred_element_type=F32)
        keep_ref[:, at] = out[:half]
        send_ref[:, at] = out[half:].astype(BF16)


def input_grad_rows(g, weight, start, rows, tile):
    depth, cols = weight.shape
    return pl.pallas_call(
        functools.partial(input_grad_kernel, start, tile),
        in_specs=[WHOLE] * 2,
        out_specs=[WHOLE] * 2,
        out_shape=[
            jax.ShapeDtypeStruct((rows // 2, depth), F32),
            jax.ShapeDtypeStruct((rows // 2, depth), BF16),
        ],
        compiler_params=params(8 * rows * tile),
        cost_estimate=cost(2 * rows * cols * depth, 2 * cols * (rows + depth)),
        name="input_grad",
    )(g, weight)


def share(total, own_ref, sends):
    rows = own_ref.shape[0]
    own_ref[...] = total(0, rows)
    for k, ref in enumerate(sends):
        ref[...] = total((k + 1) * rows, (k + 2) * rows).astype(BF16)


def core_kernel(keep_ref, got_ref, own_ref, *sends):
    share(lambda a, b: keep_ref[a:b, :] + got_ref[a:b, :].astype(F32), own_ref, sends)


def add_kernel(own_ref, *refs):
    refs[-1][...] = own_ref[...] + sum(ref[...].astype(F32) for ref in refs[:-1])


def chip_kernel(place, first_ref, second_ref, own_ref, *sends):
    bit = (lax.axis_index("vocab") >> 1) & place.bit
    group = place.group
    for zk, ref in enumerate((own_ref, *sends)):
        at = place.half_of(zk) * group
        at = slice(at, at + group)

        def put(source, ref=ref, at=at):
            ref[...] = source[at, :].astype(ref.dtype)

        pl.when(bit == zk & place.bit)(functools.partial(put, first_ref))
        pl.when(bit != zk & place.bit)(functools.partial(put, second_ref))


def small(kernel, args, shapes):
    nbytes = sum(x.size * x.dtype.itemsize for x in (*args, *shapes))
    return pl.pallas_call(
        kernel,
        in_specs=[WHOLE] * len(args),
        out_specs=[WHOLE] * len(shapes),
        out_shape=shapes,
        compiler_params=params(0),
        cost_estimate=cost(0, nbytes),
    )(*args)


def shares(rows, cols, count):
    return [jax.ShapeDtypeStruct((rows, cols), BF16 if k else F32) for k in range(count)]


def turn_kernel(place, h_ref, o_ref, h_sc):
    bit = (lax.axis_index("vocab") >> 1) & place.bit
    to = 0
    for part in range(2):
        for outer in range(place.nh * 2):
            for zk in range(place.nz):
                if zk & place.bit:
                    continue
                at = jnp.bitwise_xor(bit, zk | (part * place.bit)) & place.bit
                at = (outer * place.nz + (zk | at)) * place.group
                at = pl.ds(pl.multiple_of(at, place.group), place.group)
                h_sc[to : to + place.group, :] = h_ref[at, :]
                to += place.group
    o_ref[...] = h_sc[...].T


def turned(place, h):
    rows, depth = h.shape
    return pl.pallas_call(
        functools.partial(turn_kernel, place),
        in_specs=[WHOLE],
        out_specs=WHOLE,
        out_shape=jax.ShapeDtypeStruct((depth, rows), BF16),
        scratch_shapes=[pltpu.VMEM((rows, depth), BF16)],
        compiler_params=params(2 * rows * depth),
        cost_estimate=cost(0, 4 * rows * depth),
        name="turn",
    )(h)


def weight_grad_kernel(start, tile, ht_ref, g_ref, *refs):
    at = pl.multiple_of((start + pl.program_id(0)) * tile, tile)
    g = g_ref[:, pl.ds(at, tile)]
    refs[-1][0] = jnp.dot(ht_ref[...], g, preferred_element_type=F32).astype(BF16)


def weight_grad_part(ht, g, before, part, parts, tile):
    depth, rows = ht.shape
    cols = g.shape[1]
    steps = cols // parts // tile
    start = part * steps
    extra = [] if before is None else [before]
    return pl.pallas_call(
        functools.partial(weight_grad_kernel, start, tile),
        grid=(steps,),
        in_specs=[WHOLE] * 2 + [pl.BlockSpec(memory_space=pl.ANY)] * len(extra),
        out_specs=pl.BlockSpec((1, depth, tile), lambda j: (0, 0, start + j)),
        out_shape=jax.ShapeDtypeStruct((1, depth, cols), BF16),
        input_output_aliases={2: 0} if extra else {},
        compiler_params=params(8 * depth * tile),
        cost_estimate=cost(2 * rows * cols * depth // parts, 2 * depth * cols // parts),
        name="weight_grad",
    )(ht, g, *extra)


class Place:
    def __init__(self, nh, nv, group):
        self.nh, self.nv, self.nz, self.group = nh, nv, nv // 2, group
        self.bit = nh // 4

    def position(self, d):
        hk, vk = d // self.nv, d % self.nv
        zk, ck = vk // 2, vk % 2
        return (ck * self.nh + hk) * self.nz + zk

    def half_of(self, zk):
        return ((zk >> 1) & ~(self.bit - 1)) | (zk & (self.bit - 1))

    def half_position(self, d):
        hk, vk = d // self.nv, d % self.nv
        zk, ck = vk // 2, vk % 2
        return (ck * self.nh + hk) * (self.nz // 2) + self.half_of(zk)


def swap(x, axis, size, k):
    return lax.ppermute(x, axis, [(i, i ^ k) for i in range(size)])


def coded(i):
    return i ^ (i >> 1)


def shifted(z, nz, step):
    place, rest = z, z >> 1
    bits = nz
    while bits > 2:
        place, rest, bits = place ^ rest, rest >> 1, bits // 2
    return coded((place + step) & (nz - 1))


def relative(nh, nv, hidden, weight, teacher):
    place = Place(nh, nv, hidden.shape[0])
    nz = place.nz
    v = lax.axis_index("vocab")
    z, core = v >> 1, v & 1
    cols = weight.shape[2]

    near = [hidden] + [None] * (nz - 1)
    for k in range(nz - 1, 0, -1):
        near[k] = swap(hidden, "vocab", nv, 2 * k)

    rows = teacher.shape[1] // 2

    def piece(step, ck, part):
        to = shifted(z, nz, step) * 2 + (core ^ ck)
        return lax.dynamic_slice(teacher, (0, part * rows, to * cols), (1, rows, cols))[0]

    def move(x, step, ck):
        pairs = [
            (2 * i + c, 2 * shifted(i, nz, step) + (c ^ ck)) for i in range(nz) for c in range(2)
        ]
        return lax.ppermute(x, "vocab", pairs)

    blocks = []
    pieces = lax.optimization_barrier(
        tuple(
            tuple((piece(step, 0, part), piece(step, 1, part)) for step in range(nz))
            for part in range(2)
        )
    )
    for part in range(2):
        half = []
        for step in range(nz):
            mine, cross = pieces[part][step]
            if step:
                mine = move(mine, step, 0)
            cross = move(cross, step, 1)
            half += [mine, cross]
        blocks.append(half)

    block = stacked(near)
    own = [block]
    for k in range(1, nh):
        own.append(swap(block, "head", nh, k))
    other = []
    for k in range(nh):
        other.append(swap(own[k], "vocab", nv, 1))

    tstat, near_weight = prepared(teacher, weight[0])
    e, h, stat = student(own + other, near_weight, tstat, teacher.shape[1], 512)
    pair = swap(stat, "vocab", nv, 1)
    pair = stacked([stat, pair])
    stats = [pair]
    for k in range(1, nz):
        stats.append(swap(pair, "vocab", nv, 2 * k))
    ht = turned(place, h)

    rows, depth = place.group * nz // 2, weight.shape[1]
    g, sums = (), []
    for part in range(2):
        g = (logit_grad(place, part, stats, blocks[part], e, g, 1024),)
        start = part * e.shape[0] // 2
        keep, send = input_grad_rows(g[0], near_weight, start, e.shape[0] // 2, 512)
        send = swap(send, "vocab", nv, 1)
        own, *piece = small(core_kernel, (keep, send), shares(rows, depth, nh))
        for k in range(1, nh):
            piece[k - 1] = swap(piece[k - 1], "head", nh, k)
        sums += small(add_kernel, (own, *piece), shares(rows, depth, 1))
    kernel = functools.partial(chip_kernel, place)
    own, *piece = small(kernel, sums, shares(place.group, depth, nz))
    for k in range(1, nz):
        piece[k - 1] = swap(piece[k - 1], "vocab", nv, 2 * k)
    (total,) = small(add_kernel, (own, *piece), shares(place.group, depth, 1))
    g = g[0]
    grad = None
    for part in range(PARTS):
        grad = weight_grad_part(ht, g, grad, part, PARTS, 256)
    return (grad, total)


PARTS = 4


def gathered(hidden, weight, teacher):
    trunk = lax.all_gather(hidden, ("head", "vocab"), axis=0, tiled=True)
    weight = weight[0]
    teacher = lax.all_to_all(teacher, "vocab", split_axis=2, concat_axis=1, tiled=True)[0]
    teacher = teacher.astype(F32)
    s = jnp.dot(trunk, weight, preferred_element_type=F32)
    tops = [jnp.max(x, axis=1) for x in (s, teacher)]
    totals = [jnp.sum(jnp.exp(x - m[:, None]), axis=1) for x, m in zip((s, teacher), tops)]
    stat = lax.all_gather(jnp.stack(tops + totals), "vocab")
    prob = []
    for i, x in enumerate((s, teacher)):
        top = jnp.max(stat[:, i], axis=0)
        total = jnp.sum(stat[:, i + 2] * jnp.exp(stat[:, i] - top), axis=0)
        prob.append(jnp.exp(x - top[:, None]) / total[:, None])
    g = (prob[0] - prob[1]).astype(BF16)
    grad = lax.dot_general(trunk, g, TN, preferred_element_type=F32).astype(BF16)[None]
    back = lax.dot_general(g, weight, NT, preferred_element_type=F32)
    return (grad, lax.psum_scatter(back, ("head", "vocab"), scatter_dimension=0, tiled=True))


def per_device(nh, nv, plain, hidden, weight, teacher):
    if plain:
        return gathered(hidden, weight, teacher)
    return relative(nh, nv, hidden, weight, teacher)


def solution(mesh):
    nh, nv = mesh.shape["head"], mesh.shape["vocab"]

    def step(hidden, weight, teacher):
        group = hidden.shape[0] // (nh * nv)
        plain = nh & (nh - 1) or nv & (nv - 1) or group % 16 or not 4 <= nh < 2 * nv
        run = jax.shard_map(
            functools.partial(per_device, nh, nv, plain),
            mesh=mesh,
            in_specs=(P(("head", "vocab"), None), P("head", None, "vocab"), P("head", "vocab", None)),
            out_specs=(P("head", None, "vocab"), P(("head", "vocab"), None)),
            check_vma=False,
        )
        return run(hidden, weight, teacher)

    return step
```

```python
import functools

import jax
import jax.numpy as jnp
from jax import lax
from jax.experimental import pallas as pl
from jax.experimental.pallas import tpu as pltpu
from jax.sharding import PartitionSpec as P


F32 = jnp.float32
BF16 = jnp.bfloat16
LANES = 128
NT = (((1,), (1,)), ((), ()))
TN = (((0,), (0,)), ((), ()))
MIB = 1024 * 1024
ROOM = 42 * MIB


def params(nbytes):
    return pltpu.CompilerParams(vmem_limit_bytes=nbytes + 4 * MIB)


def cost(flops, nbytes):
    return pl.CostEstimate(flops=flops, bytes_accessed=nbytes, transcendentals=0)


WHOLE = pl.BlockSpec(memory_space=pltpu.VMEM)
STORED = pl.BlockSpec(memory_space=pltpu.HBM)


def prepare_kernel(*refs):
    pieces, (w_hbm, o_ref, w_ref, cols_sc, sem) = refs[:-5], refs[-5:]
    weight = pltpu.make_async_copy(w_hbm, w_ref, sem)
    weight.start()
    half, cols = pieces[0].shape
    cols_sc[...] = jnp.zeros_like(cols_sc)
    step = 16
    lane = lax.broadcasted_iota(jnp.int32, (step, LANES), 1)
    count = len(pieces) // 2
    for at in range(0, 2 * half, step):
        part, row = divmod(at, half)
        row = slice(row, row + step)
        views = [
            (ref, slice(c, c + LANES))
            for ref in pieces[part * count : (part + 1) * count]
            for c in range(0, cols, LANES)
        ]
        top = [jnp.full((step, LANES), -jnp.inf, F32)] * 4
        for i, (ref, c) in enumerate(views):
            top[i % 4] = jnp.maximum(top[i % 4], ref[row, c].astype(F32))
        top = jnp.max(functools.reduce(jnp.maximum, top), axis=1, keepdims=True)
        wide = jnp.broadcast_to(top, (step, LANES))
        total = [jnp.zeros((step, LANES), F32)] * 4
        for i, (ref, c) in enumerate(views):
            total[i % 4] = total[i % 4] + jnp.exp(ref[row, c].astype(F32) - wide)
        total = jnp.sum(sum(total), axis=1, keepdims=True)
        cols_sc[at : at + step, :] = jnp.where(lane == 0, wide, jnp.where(lane == 1, total, 0.0))
    o_ref[...] = cols_sc[...].T[:8, :]
    weight.wait()


def prepared(pieces, weight):
    rows, cols = pieces[0].shape
    return pl.pallas_call(
        prepare_kernel,
        in_specs=[WHOLE] * len(pieces) + [STORED],
        out_specs=[WHOLE] * 2,
        out_shape=[
            jax.ShapeDtypeStruct((8, LANES), F32),
            jax.ShapeDtypeStruct(weight.shape, BF16),
        ],
        scratch_shapes=[pltpu.VMEM((LANES, LANES), F32), pltpu.SemaphoreType.DMA],
        compiler_params=pltpu.CompilerParams(vmem_limit_bytes=ROOM),
        cost_estimate=cost(8 * rows * cols * len(pieces), 4 * weight.size),
        name="prepare",
    )(*pieces, weight)


def stack_kernel(*refs):
    rows = refs[0].shape[0]
    for i, ref in enumerate(refs[:-1]):
        refs[-1][i * rows : (i + 1) * rows, :] = ref[...]


def stacked(parts):
    rows, cols = parts[0].shape
    shape = jax.ShapeDtypeStruct((rows * len(parts), cols), parts[0].dtype)
    nbytes = shape.size * shape.dtype.itemsize
    return pl.pallas_call(
        stack_kernel,
        in_specs=[WHOLE] * len(parts),
        out_specs=WHOLE,
        out_shape=shape,
        compiler_params=params(0),
        cost_estimate=cost(0, 2 * nbytes),
    )(*parts)


def student_kernel(pieces, tile, own, *refs):
    parts, (w_ref, t_ref, e_ref, h_ref, stat_ref, s_ref, cols_sc) = refs[:pieces], refs[pieces:]
    rows = parts[0].shape[0]
    for i, part in enumerate(parts):
        h_ref[i * rows : (i + 1) * rows, :] = part[...]
    for at in range(0, w_ref.shape[1], tile):
        w = w_ref[:, at : at + tile]
        s_ref[:, at : at + tile] = jnp.dot(h_ref[...], w, preferred_element_type=F32)

    step = 8
    lane = lax.broadcasted_iota(jnp.int32, (step, LANES), 1)

    def body(i, _):
        at = pl.ds(pl.multiple_of(i * step, step), step)
        x = s_ref[at, :]
        top = jnp.max(x, axis=1, keepdims=True)
        e = jnp.exp(x - top)
        e_ref[at, :] = e
        total = jnp.sum(e, axis=1, keepdims=True)
        cols_sc[at, :] = jnp.where(lane == 0, top, jnp.where(lane == 1, total, 0.0))
        return _

    lax.fori_loop(0, e_ref.shape[0] // step, body, 0, unroll=8)
    stat_ref[...] = cols_sc[...].T[:8, :]
    stat_ref[2:4, :own] = t_ref[:2, :own]


def student(parts, weight, tstat, own, tile):
    depth, cols = weight.shape
    rows = sum(p.shape[0] for p in parts)
    return pl.pallas_call(
        functools.partial(student_kernel, len(parts), tile, own),
        in_specs=[WHOLE] * (len(parts) + 2),
        out_specs=[WHOLE] * 3,
        out_shape=[
            jax.ShapeDtypeStruct((rows, cols), F32),
            jax.ShapeDtypeStruct((rows, depth), BF16),
            jax.ShapeDtypeStruct((8, rows), F32),
        ],
        scratch_shapes=[pltpu.VMEM((rows, cols), F32), pltpu.VMEM((rows, LANES), F32)],
        compiler_params=params(4 * rows * (cols + LANES)),
        cost_estimate=cost(2 * rows * cols * depth, 2 * depth * cols + 4 * rows * cols),
        name="student",
    )(*parts, weight, tstat)


def swap_groups(x, size, lanes):
    lane = lax.broadcasted_iota(jnp.int32, x.shape, 1)
    return jnp.where((lane // size) % 2 == 0, pltpu.roll(x, lanes - size, 1), pltpu.roll(x, size, 1))


def logit_grad_kernel(place, part, n_stats, tile, *refs):
    stats = refs[:n_stats]
    teachers = refs[n_stats : n_stats + place.nv]
    e_ref, *before, g_ref, cols_sc = refs[n_stats + place.nv :]
    rows = e_ref.shape[0]
    half = rows // 2
    if part:
        g_ref[:half, :] = before[0][...]
    v = lax.axis_index("vocab")
    me = lax.axis_index("head") * place.nv + v

    tops, totals, teacher = [], [], []
    for zk, ref in enumerate(stats):
        for ck in range(2):
            x = ref[8 * ck : 8 * ck + 8, :]
            teacher.append(x[2:4, : rows // place.nv])
            if ck:
                x = jnp.concatenate([x[:, half:], x[:, :half]], axis=1)
            bit = 1
            while bit < place.nz:
                if zk & bit:
                    x = swap_groups(x, bit * place.group, rows)
                bit *= 2
            tops.append(x[0:1])
            totals.append(x[1:2])
    top = functools.reduce(jnp.maximum, tops)
    total = sum(t * jnp.exp(m - top) for m, t in zip(tops, totals))
    scale = jnp.exp(tops[0] - top) / total
    teacher = jnp.concatenate(teacher, axis=1)
    packed = jnp.concatenate(
        [scale, teacher[0:1], 1.0 / teacher[1:2], jnp.zeros((LANES - 3, rows), F32)], axis=0
    )
    cols_sc[...] = packed.T

    @pl.loop(0, g_ref.shape[1] // tile)
    def _(j):
        across = pl.ds(pl.multiple_of(j * tile, tile), tile)
        for i, t_ref in enumerate(teachers):
            step, ck = divmod(i, 2)
            per = t_ref.shape[0] // place.group
            source = shifted(v >> 1, place.nz, place.nz - step) * 2 + jnp.bitwise_xor(v & 1, ck)
            vk = jnp.bitwise_xor(source, v)
            for sub in range(per):
                can = (source * 2 + part) * per + sub
                d = jnp.bitwise_xor(me, can)
                at = pl.multiple_of(place.position(d) * place.group, place.group)
                at = pl.ds(at, place.group)
                to = pl.multiple_of(place.half_position(d) * place.group, place.group)
                to = pl.ds(part * half + to, place.group)
                c = cols_sc[at, :]
                own = pl.multiple_of(((vk * 2 + part) * per + sub) * place.group, place.group)
                own = cols_sc[pl.ds(own, place.group), :]
                t = t_ref[sub * place.group : (sub + 1) * place.group, across].astype(F32)
                q = jnp.exp(t - own[:, 1:2]) * own[:, 2:3]
                g_ref[to, across] = (e_ref[at, across] * c[:, 0:1] - q).astype(BF16)


def logit_grad(place, part, stats, teachers, e, before, tile):
    rows, cols = e.shape
    if not part:
        rows //= 2
    return pl.pallas_call(
        functools.partial(logit_grad_kernel, place, part, len(stats), tile),
        in_specs=[WHOLE] * (len(stats) + len(teachers) + 1 + len(before)),
        out_specs=WHOLE,
        out_shape=jax.ShapeDtypeStruct((rows, cols), BF16),
        scratch_shapes=[pltpu.VMEM((e.shape[0], LANES), F32)],
        compiler_params=params(4 * e.shape[0] * LANES),
        cost_estimate=cost(8 * rows * cols, 8 * rows * cols),
        name="logit_grad",
    )(*stats, *teachers, e, *before)


def input_grad_kernel(start, tile, g_ref, w_ref, keep_ref, send_ref):
    half = keep_ref.shape[0]
    g = g_ref.at[start : start + 2 * half]

    @pl.loop(0, keep_ref.shape[1] // tile)
    def _(j):
        at = pl.ds(pl.multiple_of(j * tile, tile), tile)
        out = lax.dot_general(g[...], w_ref[at, :], NT, preferred_element_type=F32)
        keep_ref[:, at] = out[:half]
        send_ref[:, at] = out[half:].astype(BF16)


def input_grad_rows(g, weight, start, rows, tile):
    depth, cols = weight.shape
    return pl.pallas_call(
        functools.partial(input_grad_kernel, start, tile),
        in_specs=[WHOLE] * 2,
        out_specs=[WHOLE] * 2,
        out_shape=[
            jax.ShapeDtypeStruct((rows // 2, depth), F32),
            jax.ShapeDtypeStruct((rows // 2, depth), BF16),
        ],
        compiler_params=params(8 * rows * tile),
        cost_estimate=cost(2 * rows * cols * depth, 2 * cols * (rows + depth)),
        name="input_grad",
    )(g, weight)


def share(total, own_ref, sends):
    rows = own_ref.shape[0]
    own_ref[...] = total(0, rows)
    for k, ref in enumerate(sends):
        ref[...] = total((k + 1) * rows, (k + 2) * rows).astype(BF16)


def core_kernel(keep_ref, got_ref, own_ref, *sends):
    share(lambda a, b: keep_ref[a:b, :] + got_ref[a:b, :].astype(F32), own_ref, sends)


def add_kernel(own_ref, *refs):
    refs[-1][...] = own_ref[...] + sum(ref[...].astype(F32) for ref in refs[:-1])


def chip_kernel(place, first_ref, second_ref, own_ref, *sends):
    bit = (lax.axis_index("vocab") >> 1) & place.bit
    group = place.group
    for zk, ref in enumerate((own_ref, *sends)):
        at = place.half_of(zk) * group
        at = slice(at, at + group)

        def put(source, ref=ref, at=at):
            ref[...] = source[at, :].astype(ref.dtype)

        pl.when(bit == zk & place.bit)(functools.partial(put, first_ref))
        pl.when(bit != zk & place.bit)(functools.partial(put, second_ref))


def small(kernel, args, shapes):
    nbytes = sum(x.size * x.dtype.itemsize for x in (*args, *shapes))
    return pl.pallas_call(
        kernel,
        in_specs=[WHOLE] * len(args),
        out_specs=[WHOLE] * len(shapes),
        out_shape=shapes,
        compiler_params=params(0),
        cost_estimate=cost(0, nbytes),
    )(*args)


def shares(rows, cols, count):
    return [jax.ShapeDtypeStruct((rows, cols), BF16 if k else F32) for k in range(count)]


def turn_kernel(place, h_ref, o_ref, h_sc):
    bit = (lax.axis_index("vocab") >> 1) & place.bit
    to = 0
    for part in range(2):
        for outer in range(place.nh * 2):
            for zk in range(place.nz):
                if zk & place.bit:
                    continue
                at = jnp.bitwise_xor(bit, zk | (part * place.bit)) & place.bit
                at = (outer * place.nz + (zk | at)) * place.group
                at = pl.ds(pl.multiple_of(at, place.group), place.group)
                h_sc[to : to + place.group, :] = h_ref[at, :]
                to += place.group
    o_ref[...] = h_sc[...].T


def turned(place, h):
    rows, depth = h.shape
    return pl.pallas_call(
        functools.partial(turn_kernel, place),
        in_specs=[WHOLE],
        out_specs=WHOLE,
        out_shape=jax.ShapeDtypeStruct((depth, rows), BF16),
        scratch_shapes=[pltpu.VMEM((rows, depth), BF16)],
        compiler_params=params(2 * rows * depth),
        cost_estimate=cost(0, 4 * rows * depth),
        name="turn",
    )(h)


def weight_grad_kernel(start, tile, ht_ref, g_ref, *refs):
    at = pl.multiple_of((start + pl.program_id(0)) * tile, tile)
    g = g_ref[:, pl.ds(at, tile)]
    refs[-1][0] = jnp.dot(ht_ref[...], g, preferred_element_type=F32).astype(BF16)


def weight_grad_part(ht, g, before, part, parts, tile):
    depth, rows = ht.shape
    cols = g.shape[1]
    steps = cols // parts // tile
    start = part * steps
    extra = [] if before is None else [before]
    return pl.pallas_call(
        functools.partial(weight_grad_kernel, start, tile),
        grid=(steps,),
        in_specs=[WHOLE] * 2 + [pl.BlockSpec(memory_space=pl.ANY)] * len(extra),
        out_specs=pl.BlockSpec((1, depth, tile), lambda j: (0, 0, start + j)),
        out_shape=jax.ShapeDtypeStruct((1, depth, cols), BF16),
        input_output_aliases={2: 0} if extra else {},
        compiler_params=params(8 * depth * tile),
        cost_estimate=cost(2 * rows * cols * depth // parts, 2 * depth * cols // parts),
        name="weight_grad",
    )(ht, g, *extra)


class Place:
    def __init__(self, nh, nv, group):
        self.nh, self.nv, self.nz, self.group = nh, nv, nv // 2, group
        self.bit = nh // 4

    def position(self, d):
        hk, vk = d // self.nv, d % self.nv
        zk, ck = vk // 2, vk % 2
        return (ck * self.nh + hk) * self.nz + zk

    def half_of(self, zk):
        return ((zk >> 1) & ~(self.bit - 1)) | (zk & (self.bit - 1))

    def half_position(self, d):
        hk, vk = d // self.nv, d % self.nv
        zk, ck = vk // 2, vk % 2
        return (ck * self.nh + hk) * (self.nz // 2) + self.half_of(zk)


def swap(x, axis, size, k):
    return lax.ppermute(x, axis, [(i, i ^ k) for i in range(size)])


def coded(i):
    return i ^ (i >> 1)


def shifted(z, nz, step):
    place, rest = z, z >> 1
    bits = nz
    while bits > 2:
        place, rest, bits = place ^ rest, rest >> 1, bits // 2
    return coded((place + step) & (nz - 1))


def relative(nh, nv, hidden, weight, teacher):
    place = Place(nh, nv, hidden.shape[0])
    nz = place.nz
    v = lax.axis_index("vocab")
    z, core = v >> 1, v & 1
    cols = weight.shape[2]

    near = [hidden] + [None] * (nz - 1)
    for k in range(nz - 1, 0, -1):
        near[k] = swap(hidden, "vocab", nv, 2 * k)

    rows = teacher.shape[1] // 2

    def piece(step, ck, part):
        to = shifted(z, nz, step) * 2 + (core ^ ck)
        return lax.dynamic_slice(teacher, (0, part * rows, to * cols), (1, rows, cols))[0]

    def move(x, step, ck):
        pairs = [
            (2 * i + c, 2 * shifted(i, nz, step) + (c ^ ck)) for i in range(nz) for c in range(2)
        ]
        return lax.ppermute(x, "vocab", pairs)

    blocks = []
    pieces = lax.optimization_barrier(
        tuple(
            tuple((piece(step, 0, part), piece(step, 1, part)) for step in range(nz))
            for part in range(2)
        )
    )
    for part in range(2):
        half = []
        for step in range(nz):
            mine, cross = pieces[part][step]
            if step:
                mine = move(mine, step, 0)
            cross = move(cross, step, 1)
            half += [mine, cross]
        blocks.append(half)

    near[0] = stacked(near[:1])
    block = stacked(near)
    own = [block]
    for k in range(1, nh):
        own.append(swap(block, "head", nh, k))
    other = []
    for k in range(nh):
        other.append(swap(own[k], "vocab", nv, 1))

    flat = [x for half in pieces for pair in half for x in pair]
    tstat, near_weight = prepared(flat, weight[0])
    e, h, stat = student(own + other, near_weight, tstat, teacher.shape[1], 1024)
    pair = swap(stat, "vocab", nv, 1)
    pair = stacked([stat, pair])
    stats = [pair]
    for k in range(1, nz):
        stats.append(swap(pair, "vocab", nv, 2 * k))
    ht = turned(place, h)

    rows, depth = place.group * nz // 2, weight.shape[1]
    g, sums = (), []
    for part in range(2):
        g = (logit_grad(place, part, stats, blocks[part], e, g, 2048),)
        start = part * e.shape[0] // 2
        keep, send = input_grad_rows(g[0], near_weight, start, e.shape[0] // 2, 2048)
        send = swap(send, "vocab", nv, 1)
        own, *piece = small(core_kernel, (keep, send), shares(rows, depth, nh))
        for k in range(1, nh):
            piece[k - 1] = swap(piece[k - 1], "head", nh, k)
        sums += small(add_kernel, (own, *piece), shares(rows, depth, 1))
    kernel = functools.partial(chip_kernel, place)
    own, *piece = small(kernel, sums, shares(place.group, depth, nz))
    for k in range(1, nz):
        piece[k - 1] = swap(piece[k - 1], "vocab", nv, 2 * k)
    (total,) = small(add_kernel, (own, *piece), shares(place.group, depth, 1))
    g = g[0]
    grad = None
    for part in range(PARTS):
        grad = weight_grad_part(ht, g, grad, part, PARTS, 512)
    return (grad, total)


PARTS = 2


def gathered(hidden, weight, teacher):
    trunk = lax.all_gather(hidden, ("head", "vocab"), axis=0, tiled=True)
    weight = weight[0]
    teacher = lax.all_to_all(teacher, "vocab", split_axis=2, concat_axis=1, tiled=True)[0]
    teacher = teacher.astype(F32)
    s = jnp.dot(trunk, weight, preferred_element_type=F32)
    tops = [jnp.max(x, axis=1) for x in (s, teacher)]
    totals = [jnp.sum(jnp.exp(x - m[:, None]), axis=1) for x, m in zip((s, teacher), tops)]
    stat = lax.all_gather(jnp.stack(tops + totals), "vocab")
    prob = []
    for i, x in enumerate((s, teacher)):
        top = jnp.max(stat[:, i], axis=0)
        total = jnp.sum(stat[:, i + 2] * jnp.exp(stat[:, i] - top), axis=0)
        prob.append(jnp.exp(x - top[:, None]) / total[:, None])
    g = (prob[0] - prob[1]).astype(BF16)
    grad = lax.dot_general(trunk, g, TN, preferred_element_type=F32).astype(BF16)[None]
    back = lax.dot_general(g, weight, NT, preferred_element_type=F32)
    return (grad, lax.psum_scatter(back, ("head", "vocab"), scatter_dimension=0, tiled=True))


def per_device(nh, nv, plain, hidden, weight, teacher):
    if plain:
        return gathered(hidden, weight, teacher)
    return relative(nh, nv, hidden, weight, teacher)


def solution(mesh):
    nh, nv = mesh.shape["head"], mesh.shape["vocab"]

    def step(hidden, weight, teacher):
        group = hidden.shape[0] // (nh * nv)
        plain = nh & (nh - 1) or nv & (nv - 1) or group % 16 or not 4 <= nh < 2 * nv
        run = jax.shard_map(
            functools.partial(per_device, nh, nv, plain),
            mesh=mesh,
            in_specs=(P(("head", "vocab"), None), P("head", None, "vocab"), P("head", "vocab", None)),
            out_specs=(P("head", None, "vocab"), P(("head", "vocab"), None)),
            check_vma=False,
        )
        return run(hidden, weight, teacher)

    return step
```
